32 devices in a mesh: gx: 4 (over z), gy: 2 (over x), gz: 4 (over y, core).
Axes of the slice: x: 2, y: 2, z: 4, core: 2. Of those that a mesh axis runs over, the one named last changes fastest.
Arguments:
- displacement: float32 [3, 32, 64, 512], P(None, 'gx', 'gy', 'gz'), may hold values from -0.1 to 0.1
- velocity: float32 [3, 32, 64, 512], P(None, 'gx', 'gy', 'gz'), may hold values from -1.55 to 1.55
- energy: float32 [32, 64, 512], P('gx', 'gy', 'gz'), may hold values from 1 to 4
- density: float32 [32, 64, 512], P('gx', 'gy', 'gz'), may hold values from 0.5 to 4
- region: int32 [32, 64, 512], P('gx', 'gy', 'gz'), may hold values from 0 to 10
- adiabatic: float32 [11], replicated, may hold values from 1.2 to 1.8
- face_flags: int32 [6], replicated, may hold values from 0 to 1
Outputs:
- final_displacement: float32 [3, 32, 64, 512], P(None, 'gx', 'gy', 'gz')
- final_velocity: float32 [3, 32, 64, 512], P(None, 'gx', 'gy', 'gz')
- final_energy: float32 [32, 64, 512], P('gx', 'gy', 'gz')
The draws below stay inside these ranges and needn't reach their ends.
Inputs may be any that keep to these rules, and one draw needn't show every extreme that they name: `face_flags`: 1 marks a symmetry plane, 0 a free surface.
All inputs are finite; a program needn't handle non-finite values.
Results may differ from the reference program's by a relative error of at most 0.0003.
Values sent between devices are 32-bit elements; how exact they have to be, the bound alone decides.
A program may use at most 64 MiB of HBM per device.

```python
import math
import jax
import jax.numpy as jnp
from jax import lax

STEPS = 2
REGIONS = 11
NX = 32
NY = 64
NZ = 512


def centred_ramp(extent, offset):
    places = (jnp.arange(extent, dtype=jnp.int32) + offset) % 6
    return places.astype(jnp.float32) - 2.5


def draw_velocity(key, part):
    phase_key = jax.random.fold_in(key, 11)
    noise_key = jax.random.fold_in(key, 12)
    phases = jax.random.randint(phase_key, (3,), 0, 6)
    ramp_slope = 0.25
    rough_part = jnp.clip(0.3 * jax.random.normal(noise_key, (3, NX, NY, NZ), jnp.float32), -0.9, 0.9)
    ramp_first = jnp.broadcast_to(centred_ramp(NX, phases[0])[:, None, None], (NX, NY, NZ))
    ramp_second = jnp.broadcast_to(centred_ramp(NY, phases[1])[None, :, None], (NX, NY, NZ))
    ramp_third = jnp.broadcast_to(centred_ramp(NZ, phases[2])[None, None, :], (NX, NY, NZ))
    converge = -ramp_slope * jnp.stack([ramp_first, ramp_second, ramp_third])
    return (converge + rough_part).astype(jnp.float32)


def touch_ends(values, key, smallest, top_value):
    index_at = [jax.random.randint(jax.random.fold_in(key, axis), (), 0, length) for axis, length in enumerate(values.shape)]
    widest = values.shape.index(max(values.shape))
    neighbour = index_at[:widest] + [(index_at[widest] + 1) % values.shape[widest]] + index_at[widest + 1:]
    return values.at[tuple(index_at)].set(smallest).at[tuple(neighbour)].set(top_value)


def steps_of(stream_key, shape, pieces, low, top_value):
    def one(axis_at, parts):
        draws = jax.random.uniform(jax.random.fold_in(jax.random.fold_in(stream_key, 6), axis_at), (parts,), jnp.float32, low / len(pieces), top_value / len(pieces))
        return jnp.repeat(jnp.exp(draws), shape[axis_at] // parts).reshape((-1,) + (1,) * (len(shape) - axis_at - 1))

    level = one(*pieces[0])
    for cut in pieces[1:]:
        level = level * one(*cut)
    return level


def normal_values(key, shape, scale, reach, split=(), kind=jnp.bfloat16):
    values = scale * jax.random.normal(key, shape, jnp.float32)
    if split:
        values = values * steps_of(key, shape, split, -0.22, 0.18)
    return jnp.clip(values, -reach, reach).astype(kind)


def setup_inputs(seed: int = 0) -> dict:
    seeds = jax.random.split(jax.random.key(seed), 8)
    displacement = normal_values(seeds[0], (3, NX, NY, NZ), 0.03, 0.1, ((1, 4), (2, 2), (3, 4)), jnp.float32)
    velocity = draw_velocity(jax.random.fold_in(seeds[7], 71), 0)
    energy = jnp.clip(jnp.exp(math.log(4.0) - 1.3862944 * jax.random.uniform(seeds[2], (NX, NY, NZ), jnp.float32) ** steps_of(seeds[2], (NX, NY, NZ), ((0, 4), (1, 2), (2, 4)), -0.2, 0.2)), 1.0, 4.0)
    density = jnp.clip(jnp.exp(math.log(4.0) - 2.0794415 * jax.random.uniform(seeds[3], (NX, NY, NZ), jnp.float32) ** steps_of(seeds[3], (NX, NY, NZ), ((0, 4), (1, 2), (2, 4)), -0.2, 0.2)), 0.5, 4.0)
    region = touch_ends(jax.random.randint(seeds[4], (NX, NY, NZ), 0, REGIONS), jax.random.fold_in(seeds[4], 1), 0, REGIONS - 1).astype(jnp.int32)
    adiabatic = jnp.clip(jax.random.uniform(seeds[5], (REGIONS,), jnp.float32, 1.2, 1.8), 1.2, 1.8)
    face_flags = touch_ends(jax.random.randint(seeds[6], (6,), 0, 2), jax.random.fold_in(seeds[6], 1), 0, 1).astype(jnp.int32)
    return dict(displacement=displacement, velocity=velocity, energy=energy, density=density, region=region, adiabatic=adiabatic, face_flags=face_flags)


COURANT = 0.25
QUAD_COEF = 1.0
LINEAR_COEF = 1.0
CORNERS = [(along_x, along_y, along_z) for along_x in (0, 1) for along_y in (0, 1) for along_z in (0, 1)]

def corner_views(extended, grid_shape):
    corner_sets = {}
    for offset in CORNERS:
        corner_sets[offset] = extended[:, offset[0]:offset[0] + grid_shape[0], offset[1]:offset[1] + grid_shape[1], offset[2]:offset[2] + grid_shape[2]]
    return corner_sets

def spread(corner_sets, start_comp):
    result = []
    for direction in range(3):
        accum = 0.0
        for offset in CORNERS:
            if offset[direction] == 1:
                accum = accum + corner_sets[offset][start_comp:start_comp + 3]
            else:
                accum = accum - corner_sets[offset][start_comp:start_comp + 3]
        result.append(0.25 * accum)
    return result

def cofactors(matrix):

    def minor_det(row_one, row_two, col_one, col_two):
        return matrix[row_one][col_one] * matrix[row_two][col_two] - matrix[row_one][col_two] * matrix[row_two][col_one]
    return [[minor_det(1, 2, 1, 2), -minor_det(1, 2, 0, 2), minor_det(1, 2, 0, 1)], [-minor_det(0, 2, 1, 2), minor_det(0, 2, 0, 2), -minor_det(0, 2, 0, 1)], [minor_det(0, 1, 1, 2), -minor_det(0, 1, 0, 2), minor_det(0, 1, 0, 1)]]

def kinematics(corner_sets):
    distorted = spread(corner_sets, 0)
    rate_terms = spread(corner_sets, 3)
    jacobian = [[distorted[direction][component] + (1.0 if component == direction else 0.0) for direction in range(3)] for component in range(3)]
    cofactor = cofactors(jacobian)
    volume = jacobian[0][0] * cofactor[0][0] + jacobian[0][1] * cofactor[0][1] + jacobian[0][2] * cofactor[0][2]
    change = 0.0
    for component in range(3):
        for direction in range(3):
            change = change + cofactor[component][direction] * rate_terms[direction][component]
    return (cofactor, volume, change / volume)

def minmod(forward, backward):
    return jnp.maximum(jnp.minimum(forward, backward), 0.0) + jnp.minimum(jnp.maximum(forward, backward), 0.0)

def face_ghosts(strain_rate, lower_rate, upper_rate, position, node_count, face_flags, dimension):
    lower_rate = jnp.where(position == 0, jnp.where(face_flags[2 * dimension] == 1, strain_rate, 0.0), lower_rate)
    upper_rate = jnp.where(position == node_count - 2, jnp.where(face_flags[2 * dimension + 1] == 1, strain_rate, 0.0), upper_rate)
    return (lower_rate, upper_rate)

def stress(strain_rate, roughness, volume, density, energy, gamma_elem, present):
    dense_now = density / volume
    length = jnp.cbrt(volume)
    compress = jnp.maximum(-strain_rate, 0.0)
    viscous = jnp.where(present, dense_now * length * length * compress * (QUAD_COEF * compress + LINEAR_COEF * roughness), 0.0)
    pressure = (gamma_elem - 1.0) * dense_now * energy
    sound_sq = gamma_elem * (gamma_elem - 1.0) * energy
    total_stress = jnp.where(present, pressure + viscous, 0.0)
    step_ratio = jnp.where(present, length / jnp.sqrt(sound_sq + viscous / dense_now), jnp.inf)
    return (total_stress, dense_now, step_ratio)

def corner_force(cofactor, total_stress, offset):
    corner_signs = [2.0 * corner_bit - 1.0 for corner_bit in offset]
    return jnp.stack([0.25 * total_stress * (corner_signs[0] * cofactor[component][0] + corner_signs[1] * cofactor[component][1] + corner_signs[2] * cofactor[component][2]) for component in range(3)])

def node_sum(term_of, grid_shape):
    accum = None
    for offset in CORNERS:
        corner_term = term_of(offset)
        padded = jnp.pad(corner_term, ((0, 0), (offset[0], 1 - offset[0]), (offset[1], 1 - offset[1]), (offset[2], 1 - offset[2])))
        accum = padded if accum is None else accum + padded
    return accum

def apply_walls(speeds, indices, counts, face_flags):
    components = []
    for dimension in range(3):
        on_wall = (indices[dimension] == 0) & (face_flags[2 * dimension] == 1) | (indices[dimension] == counts[dimension] - 1) & (face_flags[2 * dimension + 1] == 1)
        components.append(jnp.where(on_wall, 0.0, speeds[dimension]))
    return jnp.stack(components)

def reference(displacement, velocity, energy, density, region, adiabatic, face_flags):
    grid_shape = energy.shape
    indices = [jnp.arange(grid_shape[0], dtype=jnp.int32)[:, None, None], jnp.arange(grid_shape[1], dtype=jnp.int32)[None, :, None], jnp.arange(grid_shape[2], dtype=jnp.int32)[None, None, :]]
    present = (indices[0] < grid_shape[0] - 1) & (indices[1] < grid_shape[1] - 1) & (indices[2] < grid_shape[2] - 1)
    gamma_elem = adiabatic[region]
    mass_term = jnp.where(present, 0.125 * density, 0.0)[None]
    node_mass = node_sum(lambda offset: mass_term, grid_shape)[0, :grid_shape[0], :grid_shape[1], :grid_shape[2]]
    for step_index in range(STEPS):
        fields = jnp.concatenate([displacement, velocity], 0)
        extended = jnp.pad(fields, ((0, 0), (0, 1), (0, 1), (0, 1)))
        cofactor, volume, strain_rate = kinematics(corner_views(extended, grid_shape))
        roughness = 0.0
        for dimension in range(3):
            lower_pad = [(0, 0), (0, 0), (0, 0)]
            upper_pad = [(0, 0), (0, 0), (0, 0)]
            lower_pad[dimension] = (1, 0)
            upper_pad[dimension] = (0, 1)
            lower_rate = lax.slice_in_dim(jnp.pad(strain_rate, lower_pad), 0, grid_shape[dimension], axis=dimension)
            upper_rate = lax.slice_in_dim(jnp.pad(strain_rate, upper_pad), 1, grid_shape[dimension] + 1, axis=dimension)
            lower_rate, upper_rate = face_ghosts(strain_rate, lower_rate, upper_rate, indices[dimension], grid_shape[dimension], face_flags, dimension)
            roughness = roughness + jnp.abs(minmod(upper_rate - strain_rate, strain_rate - lower_rate))
        total_stress, dense_now, step_ratio = stress(strain_rate, roughness, volume, density, energy, gamma_elem, present)
        time_step = COURANT * jnp.min(step_ratio)
        force = node_sum(lambda offset: corner_force(cofactor, total_stress, offset), grid_shape)[:, :grid_shape[0], :grid_shape[1], :grid_shape[2]]
        velocity = apply_walls(velocity + time_step * force / node_mass, indices, grid_shape, face_flags)
        displacement = displacement + time_step * velocity
        energy = jnp.where(present, energy - time_step * total_stress * strain_rate / dense_now, energy)
    return (displacement, velocity, energy)
```

```python
import functools

import jax
import jax.numpy as jnp
from jax import lax
from jax.experimental import pallas as pl
from jax.experimental.pallas import tpu as pltpu
from jax.sharding import PartitionSpec as P

STEPS = 2
COURANT = 0.25
MESH = pl.DeviceIdType.MESH
AXES = ("gx", "gy", "gz")
ROWS = 8


def up8(n):
    return -(-n // 8) * 8


def kernel(sizes, shape, adi, flags, d_ref, v_ref, e_ref, rho_ref, reg_ref,
           do_ref, vo_ref, eo_ref,
           N, SYA, RYA, SZA, G, GS, T, C, VOL, GAM, ER, MA, R, SYB, RYB, SZB, RZB,
           SZC, RZC, F, SYC, RYC, RXC, INVM, ACC, SZD, RZD, DS, DRX, DRY, DRZ,
           ssem, rsem):
    X, Y, Z = shape
    XN, YN, YP = X + 1, Y + 1, Y + 8
    n_of = dict(zip(AXES, sizes))
    me = {a: lax.axis_index(a) for a in AXES}
    first = {a: me[a] == 0 for a in AXES}
    last = {a: me[a] == n_of[a] - 1 for a in AXES}
    count = [0]
    pending = []

    def remote(src, dst, axis, target):
        k = count[0]
        count[0] += 1
        return pltpu.make_async_remote_copy(
            src_ref=src, dst_ref=dst, send_sem=ssem.at[k], recv_sem=rsem.at[k],
            device_id={axis: target}, device_id_type=MESH)

    def shift(src, dst, axis, step):
        can_send = jnp.logical_not(last[axis] if step == 1 else first[axis])
        can_recv = jnp.logical_not(first[axis] if step == 1 else last[axis])
        target = jnp.clip(me[axis] + step, 0, n_of[axis] - 1)
        copy = remote(src, dst, axis, target)

        @pl.when(can_send)
        def _():
            copy.start()

        def drain():
            @pl.when(can_send)
            def _():
                copy.wait_send()

        pending.append(drain)

        def arrived():
            @pl.when(can_recv)
            def _():
                copy.wait_recv()

        return arrived

    def spread_min(tile, s, slot, axis, buf):
        n = n_of[axis]
        DS[s, slot] = tile
        copies = []
        for off in range(1, n):
            copy = remote(DS.at[s, slot], buf.at[s, off - 1], axis, lax.rem(me[axis] + off, n))
            copy.start()
            pending.append(copy.wait_send)
            copies.append(copy)

        def result():
            out = tile
            for off, copy in enumerate(copies):
                copy.wait_recv()
                out = jnp.minimum(out, buf[s, off])
            return out

        return result

    def loop(n, f):
        def step(i, carry):
            f(i)
            return carry
        lax.fori_loop(0, n, step, 0)

    barrier = pltpu.get_barrier_semaphore()
    total = 0
    for a in AXES:
        for off in range(1, n_of[a]):
            pl.semaphore_signal(barrier, inc=1,
                                device_id={a: lax.rem(me[a] + off, n_of[a])},
                                device_id_type=MESH)
            total += 1
    pl.semaphore_wait(barrier, total)

    wait_d = shift(d_ref.at[:, 0], N.at[0:3, X, 0:Y], "gx", -1)
    wait_v = shift(v_ref.at[:, 0], N.at[3:6, X, 0:Y], "gx", -1)

    lane = lax.broadcasted_iota(jnp.int32, (Y, Z), 1)
    lane_p = lax.broadcasted_iota(jnp.int32, (YP, Z), 1)
    row_p = lax.broadcasted_iota(jnp.int32, (YP, Z), 0)
    row = lax.broadcasted_iota(jnp.int32, (Y, Z), 0)
    lane_b = lax.broadcasted_iota(jnp.int32, (ROWS, Z), 1)
    row_b = lax.broadcasted_iota(jnp.int32, (ROWS, Z), 0)
    i32 = lambda b: b.astype(jnp.int32)
    far = 1 << 20
    end_x = jnp.where(last["gx"], X - 1, far)
    end_y = jnp.where(last["gy"], Y - 1, far)
    end_z = jnp.where(last["gz"], Z - 1, far)
    start_x = jnp.where(first["gx"], 0, far)
    start_y = jnp.where(first["gy"], 0, far)
    start_z = jnp.where(first["gz"], 0, far)

    def present_of(i, r0):
        edge = jnp.where(i == end_x, -1, 0)
        rb = row_b + r0
        inside = jnp.where((rb == end_y) | (lane_b == end_z), -1, 0)
        return (inside + edge) == 0

    zeros_p = jnp.zeros((YP, Z), jnp.float32)

    @pl.when(last["gx"])
    def _():
        for c in range(6):
            N[c, X] = zeros_p
        for s in range(STEPS):
            R[s, X + 1] = jnp.zeros(R.shape[2:], jnp.float32)
            for c in range(4):
                RXC[s, 1, c] = zeros_p

    @pl.when(first["gx"])
    def _():
        for s in range(STEPS):
            R[s, 0] = jnp.zeros(R.shape[2:], jnp.float32)
            for c in range(4):
                RXC[s, 0, c] = zeros_p

    @pl.when(last["gy"])
    def _():
        RYA[...] = jnp.zeros(RYA.shape, jnp.float32)
        for s in range(STEPS):
            RYB[s, 1] = jnp.zeros(RYB.shape[2:], jnp.float32)
            RYC[s, 1] = jnp.zeros(RYC.shape[2:], jnp.float32)

    @pl.when(first["gy"])
    def _():
        for s in range(STEPS):
            RYB[s, 0] = jnp.zeros(RYB.shape[2:], jnp.float32)
            RYC[s, 0] = jnp.zeros(RYC.shape[2:], jnp.float32)

    @pl.when(last["gz"])
    def _():
        G[...] = zeros_p
        RZD[...] = zeros_p
        for s in range(STEPS):
            RZB[s, 1] = jnp.zeros((Y, Z), jnp.float32)

    @pl.when(first["gz"])
    def _():
        for s in range(STEPS):
            RZB[s, 0] = jnp.zeros((Y, Z), jnp.float32)
            RZC[s] = jnp.zeros((Y, Z), jnp.float32)

    def load(i):
        for c in range(3):
            N[c, i, 0:Y] = d_ref[c, i]
            N[3 + c, i, 0:Y] = v_ref[c, i]
        reg = reg_ref[i]
        gam = jnp.zeros((Y, Z), jnp.float32)
        for k in range(adi.shape[0]):
            gam = jnp.where(reg == k, adi[k], gam)
        GAM[i] = gam
        for r0 in range(0, Y, ROWS):
            rs = slice(r0, r0 + ROWS)
            MA[i, rs] = jnp.where(present_of(i, r0), 0.125 * rho_ref[i, rs], 0.0)

    loop(X, load)

    wait_d()
    wait_v()
    for c in range(6):
        for i in range(XN):
            SYA[c * XN + i:c * XN + i + 1] = N[c, i, 0:1]
    wait = shift(SYA, RYA, "gy", -1)
    wait()
    for c in range(6):
        for i in range(XN):
            N[c, i, Y:YN] = RYA[c * XN + i:c * XN + i + 1]
    packed = zeros_p
    for c in range(6):
        for i in range(XN):
            j = c * XN + i
            value = N[c, i]
            packed = jnp.where(lane_p == j, pltpu.roll(value, j, 1) if j else value, packed)
    SZA[...] = packed
    wait = shift(SZA, G, "gz", -1)
    wait()

    for s in range(STEPS):
        final = s == STEPS - 1
        energy_ref = e_ref if s == 0 else eo_ref

        GS[0] = G[0:Y] + G[1:YN]
        GS[1] = G[1:YN] - G[0:Y]

        def plane_sums(i):
            for c in range(6):
                back = Z - 1 - (c * XN + i)
                ghost_s = pltpu.roll(GS[0], back, 1)
                ghost_d = pltpu.roll(GS[1], back, 1)
                low, high = N[c, i, 0:Y], N[c, i, 1:YN]
                ys, yd = low + high, high - low
                ys1 = jnp.where(lane == Z - 1, ghost_s, pltpu.roll(ys, Z - 1, 1))
                yd1 = jnp.where(lane == Z - 1, ghost_d, pltpu.roll(yd, Z - 1, 1))
                T[3 * c, i] = ys + ys1
                T[3 * c + 1, i] = yd + yd1
                T[3 * c + 2, i] = ys1 - ys

        loop(XN, plane_sums)

        def kinematics(i):
            for r0 in range(0, Y, ROWS):
                rs = slice(r0, r0 + ROWS)

                def grad(c):
                    return (
                        0.25 * (T[3 * c, i + 1, rs] - T[3 * c, i, rs]),
                        0.25 * (T[3 * c + 1, i + 1, rs] + T[3 * c + 1, i, rs]),
                        0.25 * (T[3 * c + 2, i + 1, rs] + T[3 * c + 2, i, rs]),
                    )

                jac = [list(grad(c)) for c in range(3)]
                for c in range(3):
                    jac[c][c] = jac[c][c] + 1.0

                def minor(r1, r2, c1, c2):
                    return jac[r1][c1] * jac[r2][c2] - jac[r1][c2] * jac[r2][c1]

                cof = [
                    [minor(1, 2, 1, 2), minor(1, 2, 2, 0), minor(1, 2, 0, 1)],
                    [minor(2, 0, 1, 2), minor(2, 0, 2, 0), minor(2, 0, 0, 1)],
                    [minor(0, 1, 1, 2), minor(0, 1, 2, 0), minor(0, 1, 0, 1)],
                ]
                volume = jac[0][0] * cof[0][0] + jac[0][1] * cof[0][1] + jac[0][2] * cof[0][2]
                change = 0.0
                for c in range(3):
                    rate = grad(3 + c)
                    for e in range(3):
                        change = change + cof[c][e] * rate[e]
                        C[3 * c + e, i, rs] = cof[c][e]
                VOL[i, rs] = volume
                R[s, i + 1, 8 + r0:8 + r0 + ROWS] = change / volume

        loop(X, kinematics)

        own = slice(8, 8 + Y)
        waits = [
            shift(R.at[s, X, own], R.at[s, 0, own], "gx", 1),
            shift(R.at[s, 1, own], R.at[s, X + 1, own], "gx", -1),
        ]
        for i in range(X):
            SYB[s, 0, i:i + 1] = R[s, i + 1, 7 + Y:8 + Y]
            SYB[s, 1, i:i + 1] = R[s, i + 1, 8:9]
        waits += [
            shift(SYB.at[s, 0], RYB.at[s, 0], "gy", 1),
            shift(SYB.at[s, 1], RYB.at[s, 1], "gy", -1),
        ]
        to_up = to_down = jnp.zeros((Y, Z), jnp.float32)
        for i in range(X):
            value = R[s, i + 1, own]
            to_up = jnp.where(lane == i, pltpu.roll(value, i + 1, 1), to_up)
            to_down = jnp.where(lane == i, pltpu.roll(value, i, 1) if i else value, to_down)
        SZB[s, 0] = to_up
        SZB[s, 1] = to_down
        waits += [
            shift(SZB.at[s, 0], RZB.at[s, 0], "gz", 1),
            shift(SZB.at[s, 1], RZB.at[s, 1], "gz", -1),
        ]
        for w in waits:
            w()
        for i in range(X):
            R[s, i + 1, 7:8] = RYB[s, 0, i:i + 1]
            R[s, i + 1, 8 + Y:9 + Y] = RYB[s, 1, i:i + 1]

        is_one = [jnp.where(flags[k] == 1, 1.0, 0.0) for k in range(6)]

        def stresses(i, least):
            low_x, high_x = i == start_x, i == end_x - 1
            for r0 in range(0, Y, ROWS):
                rs = slice(r0, r0 + ROWS)
                rr = slice(8 + r0, 8 + r0 + ROWS)
                rate = R[s, i + 1, rr]
                rb = row_b + r0
                present = present_of(i, r0)
                xl = jnp.where(low_x, is_one[0] * rate, R[s, i, rr])
                xu = jnp.where(high_x, is_one[1] * rate, R[s, i + 2, rr])
                yl = jnp.where(rb == start_y, is_one[2] * rate,
                               R[s, i + 1, 7 + r0:7 + r0 + ROWS])
                yu = jnp.where(rb == end_y - 1, is_one[3] * rate,
                               R[s, i + 1, 9 + r0:9 + r0 + ROWS])
                ghost_l = pltpu.roll(RZB[s, 0, rs], lax.rem(Z - i, Z), 1)
                ghost_u = pltpu.roll(RZB[s, 1, rs], Z - 1 - i, 1)
                zl = jnp.where(lane_b == 0, ghost_l, pltpu.roll(rate, 1, 1))
                zu = jnp.where(lane_b == Z - 1, ghost_u, pltpu.roll(rate, Z - 1, 1))
                zl = jnp.where(lane_b == start_z, is_one[4] * rate, zl)
                zu = jnp.where(lane_b == end_z - 1, is_one[5] * rate, zu)
                rough = 0.0
                for lo, hi in ((xl, xu), (yl, yu), (zl, zu)):
                    f, g = hi - rate, rate - lo
                    rough = rough + jnp.abs(
                        jnp.maximum(jnp.minimum(f, g), 0.0) + jnp.minimum(jnp.maximum(f, g), 0.0))
                volume = VOL[i, rs]
                size = jnp.exp(jnp.log(jnp.abs(volume)) * (1.0 / 3.0))
                gam, energy = GAM[i, rs], energy_ref[i, rs]
                compress = jnp.maximum(-rate, 0.0)
                visc = size * size * compress * (compress + rough)
                ge = (gam - 1.0) * energy
                work = jnp.where(present, ge + visc, 0.0)
                signed = jnp.where(volume < 0.0, -size, size)
                ratio = signed * lax.rsqrt(gam * ge + visc)
                least = jnp.minimum(least, jnp.where(present, ratio, jnp.inf))
                ER[i, rs] = jnp.where(present, work * rate, 0.0)
                quarter = jnp.where(present, 0.25 * work * rho_ref[i, rs] / volume, 0.0)
                for q in range(9):
                    C[q, i, rs] = jnp.where(present, quarter * C[q, i, rs], 0.0)
            return least

        least = lax.fori_loop(0, X, stresses, jnp.full((ROWS, Z), jnp.inf, jnp.float32))

        min_z = spread_min(least, s, 0, "gz", DRZ)
        parts = 9 if s else 10

        def column_pack(i, packed):
            for q in range(parts):
                value = C[q, i] if q < 9 else MA[i]
                packed = jnp.where(lane == q * X + i, pltpu.roll(value, q * X + i + 1, 1), packed)
            return packed

        SZC[s] = lax.fori_loop(0, X, column_pack, jnp.zeros((Y, Z), jnp.float32))
        wait = shift(SZC.at[s], RZC.at[s], "gz", 1)
        wait()
        comps = 3 if s else 4
        for c in range(comps):
            F[s, c, 0] = zeros_p

        def node_sums(i):
            def below(q):
                value = C[q, i] if q < 9 else MA[i]
                ghost = pltpu.roll(RZC[s], lax.rem(Z - (q * X + i), Z), 1)
                return value, jnp.where(lane == 0, ghost, pltpu.roll(value, 1, 1))

            def rows_of(value):
                moved = pltpu.roll(value, 1, 0)
                return jnp.where(row == 0, 0.0, moved), moved[0:1]

            for c in range(comps):
                if c < 3:
                    a, a1 = below(3 * c)
                    p = a + a1
                    a, a1 = below(3 * c + 1)
                    q = a + a1
                    a, a1 = below(3 * c + 2)
                    r = a1 - a
                    pm, p_end = rows_of(p)
                    qm, q_end = rows_of(q)
                    rm, r_end = rows_of(r)
                    u, u_end = p + pm, p_end
                    v, v_end = (qm - q) + (r + rm), q_end + r_end
                    to_low, to_low_end = v - u, v_end - u_end
                    to_high, to_high_end = v + u, v_end + u_end
                else:
                    a, a1 = below(9)
                    p = a + a1
                    pm, p_end = rows_of(p)
                    to_low = to_high = p + pm
                    to_low_end = to_high_end = p_end
                F[s, c, i, 0:Y] = F[s, c, i, 0:Y] + to_low
                F[s, c, i, Y:YN] = F[s, c, i, Y:YN] + to_low_end
                F[s, c, i + 1, 0:Y] = to_high
                F[s, c, i + 1, Y:YN] = to_high_end

        loop(X, node_sums)

        min_y = spread_min(min_z(), s, 1, "gy", DRY)
        for c in range(comps):
            for i in range(XN):
                j = c * XN + i
                SYC[s, 0, j:j + 1] = F[s, c, i, Y:YN]
                if not final:
                    SYC[s, 1, j:j + 1] = F[s, c, i, 0:1]
        waits = [shift(SYC.at[s, 0], RYC.at[s, 0], "gy", 1)]
        if not final:
            waits.append(shift(SYC.at[s, 1], RYC.at[s, 1], "gy", -1))
        for w in waits:
            w()
        for c in range(comps):
            for i in range(XN):
                j = c * XN + i
                F[s, c, i, 0:1] = F[s, c, i, 0:1] + RYC[s, 0, j:j + 1]
                if not final:
                    F[s, c, i, Y:YN] = F[s, c, i, Y:YN] + RYC[s, 1, j:j + 1]

        waits = [shift(F.at[s, 0:comps, X], RXC.at[s, 0, 0:comps], "gx", 1)]
        if not final:
            waits.append(shift(F.at[s, 0:comps, 0], RXC.at[s, 1, 0:comps], "gx", -1))
        min_x = spread_min(min_y(), s, 2, "gx", DRX)
        for w in waits:
            w()

        def total_of(c, i):
            value = F[s, c, i]
            if isinstance(i, int) and i == 0:
                value = value + RXC[s, 0, c]
            if isinstance(i, int) and i == X and not final:
                value = value + RXC[s, 1, c]
            return value

        def accelerate(i):
            if s == 0:
                mass = total_of(3, i)
                inverse = jnp.where(mass > 0.0, 1.0 / mass, 0.0)
                INVM[i] = inverse
            else:
                inverse = INVM[i]
            for c in range(3):
                ACC[c, i] = total_of(c, i) * inverse

        for i in range(X if final else XN):
            accelerate(i)

        if not final:
            packed = zeros_p
            for c in range(3):
                for i in range(XN):
                    j = (3 + c) * XN + i
                    packed = jnp.where(lane_p == j, pltpu.roll(ACC[c, i], j, 1), packed)
            SZD[...] = packed
            wait = shift(SZD, RZD, "gz", -1)
        dt = COURANT * jnp.min(min_x())

        one = [flags[k] == 1 for k in range(6)]
        wall_x0 = jnp.where(one[0], start_x, far)
        wall_x1 = jnp.where(one[1], end_x, far)
        wall_y0 = jnp.where(one[2], start_y, far)
        wall_y1 = jnp.where(one[3], end_y, far)
        wall_z0 = jnp.where(one[4], start_z, far)
        wall_z1 = jnp.where(one[5], end_z, far)
        rows = Y if final else YP
        row_n, lane_n = (row, lane) if final else (row_p, lane_p)

        def move(i):
            for c in range(3):
                speed = N[3 + c, i, 0:rows] + dt * ACC[c, i, 0:rows]
                if c == 0:
                    on_wall = (i == wall_x0) | (i == wall_x1)
                elif c == 1:
                    on_wall = (row_n == wall_y0) | (row_n == wall_y1)
                else:
                    on_wall = (lane_n == wall_z0) | (lane_n == wall_z1)
                speed = jnp.where(on_wall, 0.0, speed)
                place = N[c, i, 0:rows] + dt * speed
                if final:
                    vo_ref[c, i] = speed
                    do_ref[c, i] = place
                else:
                    N[3 + c, i] = speed
                    N[c, i] = place

        loop(X if final else XN, move)

        def heat(i):
            eo_ref[i] = energy_ref[i] - dt * ER[i]

        loop(X, heat)

        if not final:
            wait()
            ghosts = G[...]
            speed = ghosts + dt * RZD[...]
            base = 3 * XN
            on_x = (lane_p == base + wall_x0) | (lane_p == base + wall_x1)
            on_y = (lane_p >= base + XN) & (lane_p < base + 2 * XN) & (
                (row_p == wall_y0) | (row_p == wall_y1))
            speed = jnp.where(on_x | on_y, 0.0, speed)
            place = ghosts + dt * pltpu.roll(speed, Z - base, 1)
            G[...] = jnp.where(lane_p < base, place, speed)

    for drain in pending:
        drain()


def solution(mesh):
    sizes = tuple(mesh.shape[a] for a in AXES)

    def body(displacement, velocity, energy, density, region, adiabatic, face_flags):
        X, Y, Z = shape = energy.shape
        XN, YP = X + 1, Y + 8
        f32 = jnp.float32
        vm = lambda *dims: pltpu.VMEM(dims, f32)
        copies = 4 + STEPS * (6 + 5 + sum(n - 1 for n in sizes)) + 1
        scratch = [
            vm(6, XN, YP, Z), vm(up8(6 * XN), Z), vm(up8(6 * XN), Z), vm(YP, Z), vm(YP, Z),
            vm(2, Y, Z), vm(18, XN, Y, Z), vm(9, X, Y, Z), vm(X, Y, Z), vm(X, Y, Z),
            vm(X, Y, Z), vm(X, Y, Z), vm(STEPS, X + 2, Y + 16, Z),
            vm(STEPS, 2, up8(X), Z), vm(STEPS, 2, up8(X), Z),
            vm(STEPS, 2, Y, Z), vm(STEPS, 2, Y, Z),
            vm(STEPS, Y, Z), vm(STEPS, Y, Z), vm(STEPS, 4, XN, YP, Z),
            vm(STEPS, 2, up8(4 * XN), Z), vm(STEPS, 2, up8(4 * XN), Z),
            vm(STEPS, 2, 4, YP, Z), vm(XN, YP, Z), vm(3, XN, YP, Z), vm(YP, Z), vm(YP, Z),
            vm(STEPS, 3, ROWS, Z),
            vm(STEPS, max(1, sizes[0] - 1), ROWS, Z),
            vm(STEPS, max(1, sizes[1] - 1), ROWS, Z),
            vm(STEPS, max(1, sizes[2] - 1), ROWS, Z),
            pltpu.SemaphoreType.DMA((copies,)), pltpu.SemaphoreType.DMA((copies,)),
        ]
        spec_v = pl.BlockSpec(memory_space=pltpu.VMEM)
        spec_s = pl.BlockSpec(memory_space=pltpu.SMEM)
        node = jax.ShapeDtypeStruct(displacement.shape, f32)
        return pl.pallas_call(
            functools.partial(kernel, sizes, shape),
            out_shape=(node, node, jax.ShapeDtypeStruct(energy.shape, f32)),
            in_specs=[spec_s, spec_s] + [spec_v] * 5,
            out_specs=(spec_v, spec_v, spec_v),
            scratch_shapes=scratch,
            compiler_params=pltpu.CompilerParams(
                collective_id=0, has_side_effects=True, vmem_limit_bytes=48 * 1024 * 1024),
        )(adiabatic, face_flags, displacement, velocity, energy, density, region)

    node = P(None, "gx", "gy", "gz")
    elem = P("gx", "gy", "gz")
    return jax.shard_map(
        body, mesh=mesh,
        in_specs=(node, node, elem, elem, elem, P(), P()),
        out_specs=(node, node, elem), check_vma=False)
```

```python
import functools

import jax
import jax.numpy as jnp
from jax import lax
from jax.experimental import pallas as pl
from jax.experimental.pallas import tpu as pltpu
from jax.sharding import PartitionSpec as P

STEPS = 2
COURANT = 0.25
MESH = pl.DeviceIdType.MESH
AXES = ("gx", "gy", "gz")
ROWS = 8


def up8(n):
    return -(-n // 8) * 8


def kernel(sizes, shape, adi_ref, flags_ref, d_ref, v_ref, e_ref, rho_ref, reg_ref,
           do_ref, vo_ref, eo_ref,
           N, RHO, REG, adi, flags, G, GS, T, C, VOL, GAM, ER, MA, R, SYB, RYB, SZB, RZB,
           INVM, ACC, F, SY, RY, SXY, RXY, SZ, RZ, RXZ, FSY, FRY, FSXY, FRXY, FSZ, FRZ, FRXZ,
           FRX, DS, DRP, DRX, ssem, rsem, lsem):
    X, Y, Z = shape
    XN, YN, YP = X + 1, Y + 1, Y + 8
    n_of = dict(zip(AXES, sizes))
    me = {a: lax.axis_index(a) for a in AXES}
    first = {a: me[a] == 0 for a in AXES}
    last = {a: me[a] == n_of[a] - 1 for a in AXES}
    count = [0]
    pending = []

    def remote(src, dst, target):
        k = count[0]
        count[0] += 1
        return pltpu.make_async_remote_copy(
            src_ref=src, dst_ref=dst, send_sem=ssem.at[k], recv_sem=rsem.at[k],
            device_id=target, device_id_type=MESH)

    def any_of(ends, axes):
        out = ends[axes[0]]
        for a in axes[1:]:
            out = jnp.logical_or(out, ends[a])
        return out

    def shift(src, dst, axes, step):
        can_send = jnp.logical_not(any_of(last if step == 1 else first, axes))
        can_recv = jnp.logical_not(any_of(first if step == 1 else last, axes))
        copy = remote(src, dst, {a: jnp.clip(me[a] + step, 0, n_of[a] - 1) for a in axes})

        @pl.when(can_send)
        def _():
            copy.start()

        def drain():
            @pl.when(can_send)
            def _():
                copy.wait_send()

        pending.append(drain)

        def arrived():
            @pl.when(can_recv)
            def _():
                copy.wait_recv()

        return arrived

    plane_group = [{"gy": lax.rem(me["gy"] + b, n_of["gy"]), "gz": lax.rem(me["gz"] + c, n_of["gz"])}
                   for b in range(n_of["gy"]) for c in range(n_of["gz"]) if b or c]
    line_group = [{"gx": lax.rem(me["gx"] + a, n_of["gx"])} for a in range(1, n_of["gx"])]

    def spread_min(tile, s, slot, targets, buf):
        DS[s, slot] = tile
        copies = []
        for k, target in enumerate(targets):
            copy = remote(DS.at[s, slot], buf.at[s, k], target)
            copy.start()
            pending.append(copy.wait_send)
            copies.append(copy)

        def result():
            out = tile
            for k, copy in enumerate(copies):
                copy.wait_recv()
                out = jnp.minimum(out, buf[s, k])
            return out

        return result

    def loop(n, f):
        def step(i, carry):
            f(i)
            return carry
        lax.fori_loop(0, n, step, 0)

    locals_ = [
        pltpu.make_async_copy(src, dst, lsem.at[k]) for k, (src, dst) in enumerate((
            (d_ref, N.at[0:3, 0:X, 0:Y]), (v_ref, N.at[3:6, 0:X, 0:Y]),
            (rho_ref, RHO), (reg_ref, REG), (adi_ref, adi), (flags_ref, flags), (e_ref, eo_ref)))
    ]
    for copy in locals_:
        copy.start()

    barrier = pltpu.get_barrier_semaphore()
    partners = plane_group + line_group
    for step in (1, -1):
        for axes in (("gx", "gy"), ("gx", "gz"), AXES):
            partners.append({a: lax.rem(me[a] + n_of[a] + step, n_of[a]) for a in axes})
    for target in partners:
        pl.semaphore_signal(barrier, inc=1, device_id=target, device_id_type=MESH)
    pl.semaphore_wait(barrier, len(partners))

    node_waits = [shift(d_ref.at[:, 0], N.at[0:3, X, 0:Y], ("gx",), -1),
                  shift(v_ref.at[:, 0], N.at[3:6, X, 0:Y], ("gx",), -1)]

    lane = lax.broadcasted_iota(jnp.int32, (Y, Z), 1)
    lane_p = lax.broadcasted_iota(jnp.int32, (YP, Z), 1)
    row_p = lax.broadcasted_iota(jnp.int32, (YP, Z), 0)
    row = lax.broadcasted_iota(jnp.int32, (Y, Z), 0)
    lane_b = lax.broadcasted_iota(jnp.int32, (ROWS, Z), 1)
    row_b = lax.broadcasted_iota(jnp.int32, (ROWS, Z), 0)
    i32 = lambda b: b.astype(jnp.int32)
    far = 1 << 20
    end_x = jnp.where(last["gx"], X - 1, far)
    end_y = jnp.where(last["gy"], Y - 1, far)
    end_z = jnp.where(last["gz"], Z - 1, far)
    start_x = jnp.where(first["gx"], 0, far)
    start_y = jnp.where(first["gy"], 0, far)
    start_z = jnp.where(first["gz"], 0, far)

    def present_of(i, r0):
        edge = jnp.where(i == end_x, -1, 0)
        rb = row_b + r0
        inside = jnp.where((rb == end_y) | (lane_b == end_z), -1, 0)
        return (inside + edge) == 0

    zeros_p = jnp.zeros((YP, Z), jnp.float32)
    last_lane = lane_p == X
    first_lane = lane_p == 0
    for c in range(1, 6):
        last_lane = last_lane | (lane_p == c * XN + X)

    def clear(condition, *places):
        @pl.when(condition)
        def _():
            for ref, index in places:
                ref[index] = jnp.zeros(ref[index].shape, jnp.float32)

    steps = range(STEPS)
    low_rows, high_rows = slice(0, Y), slice(Y, YP)
    clear(last["gx"], *[(N, (c, X)) for c in range(6)], *[(ACC, (c, X)) for c in range(3)],
          *[(R, (s, X + 1)) for s in steps])
    clear(first["gx"], *[(R, (s, 0)) for s in steps],
          *[(FRX, (s, c)) for s in steps for c in range(4)])
    clear(last["gy"], *[(RY, (k,)) for k in range(2)], *[(RYB, (s, 1)) for s in steps])
    clear(first["gy"], *[(RYB, (s, 0)) for s in steps], *[(FRY, (s,)) for s in steps])
    clear(last["gz"], *[(RZ, (k, low_rows)) for k in range(2)], *[(RZB, (s, 1)) for s in steps])
    clear(first["gz"], *[(RZB, (s, 0)) for s in steps], *[(FRZ, (s, low_rows)) for s in steps])
    for axes, down, rows_down, up, rows_up in (
            (("gx", "gy"), RXY, None, FRXY, None),
            (("gx", "gz"), RXZ, low_rows, FRXZ, low_rows),
            (("gy", "gz"), RZ, high_rows, FRZ, high_rows),
            (AXES, RXZ, high_rows, FRXZ, high_rows)):
        at = lambda k, rows: (k,) if rows is None else (k, rows)
        clear(any_of(last, axes), *[(down, at(k, rows_down)) for k in range(2)])
        clear(any_of(first, axes), *[(up, at(s, rows_up)) for s in steps])

    def ghosts_down(ref, k, comps, base):
        for c in range(comps):
            for i in range(X):
                SY[k, c * X + i:c * X + i + 1] = ref[c, i, 0:1]
            SXY[k, c:c + 1] = ref[c, 0, 0:1]
        waits = [shift(SY.at[k, 0:up8(comps * X)], RY.at[k, 0:up8(comps * X)], ("gy",), -1),
                 shift(SXY.at[k], RXY.at[k], ("gx", "gy"), -1)]
        packed = jnp.zeros((Y, Z), jnp.float32)
        for c in range(comps):
            for i in range(XN):
                j = (base + c) * XN + i
                value = ref[c, i % X, 0:Y]
                packed = jnp.where(lane == j, pltpu.roll(value, j, 1) if j else value, packed)
        SZ[k, 0:Y] = packed
        SZ[k, Y:YP] = packed[0:8]
        waits += [shift(SZ.at[k, rows], into.at[k, rows], axes, -1)
                  for axes, into, rows in ((("gx", "gz"), RXZ, low_rows), (AXES, RXZ, high_rows),
                                           (("gy", "gz"), RZ, high_rows), (("gz",), RZ, low_rows))]

        def finish():
            for w in waits:
                w()
            for c in range(comps):
                for i in range(X):
                    ref[c, i, Y:YN] = RY[k, c * X + i:c * X + i + 1]
                ref[c, X, Y:YN] = RXY[k, c:c + 1]
            return jnp.where(last_lane, RXZ[k], RZ[k])

        return finish

    locals_[0].wait()
    locals_[1].wait()
    node_ghosts = ghosts_down(N, 0, 6, 0)
    for copy in locals_[2:]:
        copy.wait()

    def load(i):
        reg = REG[i]
        gam = jnp.zeros((Y, Z), jnp.float32)
        for k in range(adi.shape[0]):
            gam = jnp.where(reg == k, adi[k], gam)
        GAM[i] = gam
        for r0 in range(0, Y, ROWS):
            rs = slice(r0, r0 + ROWS)
            MA[i, rs] = jnp.where(present_of(i, r0), 0.125 * RHO[i, rs], 0.0)

    loop(X, load)
    for w in node_waits:
        w()
    G[...] = node_ghosts()

    for s in range(STEPS):
        final = s == STEPS - 1

        GS[0] = G[0:Y] + G[1:YN]
        GS[1] = G[1:YN] - G[0:Y]

        def plane_sums(i):
            for c in range(6):
                back = Z - 1 - (c * XN + i)
                ghost_s = pltpu.roll(GS[0], back, 1)
                ghost_d = pltpu.roll(GS[1], back, 1)
                low, high = N[c, i, 0:Y], N[c, i, 1:YN]
                ys, yd = low + high, high - low
                ys1 = jnp.where(lane == Z - 1, ghost_s, pltpu.roll(ys, Z - 1, 1))
                yd1 = jnp.where(lane == Z - 1, ghost_d, pltpu.roll(yd, Z - 1, 1))
                T[3 * c, i] = ys + ys1
                T[3 * c + 1, i] = yd + yd1
                T[3 * c + 2, i] = ys1 - ys

        loop(XN, plane_sums)

        def kinematics(i):
            for r0 in range(0, Y, ROWS):
                rs = slice(r0, r0 + ROWS)

                def grad(c):
                    return (
                        0.25 * (T[3 * c, i + 1, rs] - T[3 * c, i, rs]),
                        0.25 * (T[3 * c + 1, i + 1, rs] + T[3 * c + 1, i, rs]),
                        0.25 * (T[3 * c + 2, i + 1, rs] + T[3 * c + 2, i, rs]),
                    )

                jac = [list(grad(c)) for c in range(3)]
                for c in range(3):
                    jac[c][c] = jac[c][c] + 1.0

                def minor(r1, r2, c1, c2):
                    return jac[r1][c1] * jac[r2][c2] - jac[r1][c2] * jac[r2][c1]

                cof = [
                    [minor(1, 2, 1, 2), minor(1, 2, 2, 0), minor(1, 2, 0, 1)],
                    [minor(2, 0, 1, 2), minor(2, 0, 2, 0), minor(2, 0, 0, 1)],
                    [minor(0, 1, 1, 2), minor(0, 1, 2, 0), minor(0, 1, 0, 1)],
                ]
                volume = jac[0][0] * cof[0][0] + jac[0][1] * cof[0][1] + jac[0][2] * cof[0][2]
                change = 0.0
                for c in range(3):
                    rate = grad(3 + c)
                    for e in range(3):
                        change = change + cof[c][e] * rate[e]
                        C[3 * c + e, i, rs] = cof[c][e]
                VOL[i, rs] = volume
                R[s, i + 1, 8 + r0:8 + r0 + ROWS] = change / volume

        loop(X, kinematics)

        own = slice(8, 8 + Y)
        waits = [
            shift(R.at[s, X, own], R.at[s, 0, own], ("gx",), 1),
            shift(R.at[s, 1, own], R.at[s, X + 1, own], ("gx",), -1),
        ]
        for i in range(X):
            SYB[s, 0, i:i + 1] = R[s, i + 1, 7 + Y:8 + Y]
            SYB[s, 1, i:i + 1] = R[s, i + 1, 8:9]
        waits += [
            shift(SYB.at[s, 0], RYB.at[s, 0], ("gy",), 1),
            shift(SYB.at[s, 1], RYB.at[s, 1], ("gy",), -1),
        ]
        to_up = to_down = jnp.zeros((Y, Z), jnp.float32)
        for i in range(X):
            value = R[s, i + 1, own]
            to_up = jnp.where(lane == i, pltpu.roll(value, i + 1, 1), to_up)
            to_down = jnp.where(lane == i, pltpu.roll(value, i, 1) if i else value, to_down)
        SZB[s, 0] = to_up
        SZB[s, 1] = to_down
        waits += [
            shift(SZB.at[s, 0], RZB.at[s, 0], ("gz",), 1),
            shift(SZB.at[s, 1], RZB.at[s, 1], ("gz",), -1),
        ]
        for w in waits:
            w()
        for i in range(X):
            R[s, i + 1, 7:8] = RYB[s, 0, i:i + 1]
            R[s, i + 1, 8 + Y:9 + Y] = RYB[s, 1, i:i + 1]

        is_one = [jnp.where(flags[k] == 1, 1.0, 0.0) for k in range(6)]

        def stresses(i, least):
            low_x, high_x = i == start_x, i == end_x - 1
            for r0 in range(0, Y, ROWS):
                rs = slice(r0, r0 + ROWS)
                rr = slice(8 + r0, 8 + r0 + ROWS)
                rate = R[s, i + 1, rr]
                rb = row_b + r0
                present = present_of(i, r0)
                xl = jnp.where(low_x, is_one[0] * rate, R[s, i, rr])
                xu = jnp.where(high_x, is_one[1] * rate, R[s, i + 2, rr])
                yl = jnp.where(rb == start_y, is_one[2] * rate,
                               R[s, i + 1, 7 + r0:7 + r0 + ROWS])
                yu = jnp.where(rb == end_y - 1, is_one[3] * rate,
                               R[s, i + 1, 9 + r0:9 + r0 + ROWS])
                ghost_l = pltpu.roll(RZB[s, 0, rs], lax.rem(Z - i, Z), 1)
                ghost_u = pltpu.roll(RZB[s, 1, rs], Z - 1 - i, 1)
                zl = jnp.where(lane_b == 0, ghost_l, pltpu.roll(rate, 1, 1))
                zu = jnp.where(lane_b == Z - 1, ghost_u, pltpu.roll(rate, Z - 1, 1))
                zl = jnp.where(lane_b == start_z, is_one[4] * rate, zl)
                zu = jnp.where(lane_b == end_z - 1, is_one[5] * rate, zu)
                rough = 0.0
                for lo, hi in ((xl, xu), (yl, yu), (zl, zu)):
                    f, g = hi - rate, rate - lo
                    rough = rough + jnp.abs(
                        jnp.maximum(jnp.minimum(f, g), 0.0) + jnp.minimum(jnp.maximum(f, g), 0.0))
                volume = VOL[i, rs]
                size = jnp.exp(jnp.log(jnp.abs(volume)) * (1.0 / 3.0))
                gam, energy = GAM[i, rs], eo_ref[i, rs]
                compress = jnp.maximum(-rate, 0.0)
                visc = size * size * compress * (compress + rough)
                ge = (gam - 1.0) * energy
                work = jnp.where(present, ge + visc, 0.0)
                signed = jnp.where(volume < 0.0, -size, size)
                ratio = signed * lax.rsqrt(gam * ge + visc)
                least = jnp.minimum(least, jnp.where(present, ratio, jnp.inf))
                ER[i, rs] = jnp.where(present, work * rate, 0.0)
                quarter = jnp.where(present, 0.25 * work * RHO[i, rs] / volume, 0.0)
                for q in range(9):
                    C[q, i, rs] = jnp.where(present, quarter * C[q, i, rs], 0.0)
            return least

        least = lax.fori_loop(0, X, stresses, jnp.full((ROWS, Z), jnp.inf, jnp.float32))

        plane_min = spread_min(least, s, 0, plane_group, DRP)
        comps = 3 if s else 4

        def column_pack(i, tiles):
            out = []
            for part, tile in enumerate(tiles):
                for c in range(comps):
                    if c == 3 and part != 2:
                        continue
                    value = MA[i] if c == 3 else C[3 * c + part, i]
                    j = c * XN + i
                    tile = jnp.where(lane == j, pltpu.roll(value, lax.rem(j + 1, Z), 1), tile)
                out.append(tile)
            return tuple(out)

        tiles = lax.fori_loop(0, X, column_pack, (jnp.zeros((Y, Z), jnp.float32),) * 3)
        p, q, r = [jnp.concatenate([t, jnp.zeros((8, Z), jnp.float32)], 0) for t in tiles]
        pm, qm, rm = [pltpu.roll(t, 1, 0) for t in (p, q, r)]
        u, v = p + pm, (qm - q) + (r + rm)
        FSZ[s] = (v - u) + pltpu.roll(v + u, 1, 1)
        waits = [shift(FSZ.at[s, rows], into.at[s, rows], axes, 1)
                 for axes, into, rows in ((AXES, FRXZ, high_rows), (("gx", "gz"), FRXZ, low_rows),
                                          (("gy", "gz"), FRZ, high_rows), (("gz",), FRZ, low_rows))]

        def node_sums(i, top):
            def below(q):
                value = C[q, i] if q < 9 else MA[i]
                return value, jnp.where(lane == 0, 0.0, pltpu.roll(value, 1, 1))

            def rows_of(value):
                moved = pltpu.roll(value, 1, 0)
                return jnp.where(row == 0, 0.0, moved), moved[0:1]

            for c in range(comps):
                if c < 3:
                    a, a1 = below(3 * c)
                    p = a + a1
                    a, a1 = below(3 * c + 1)
                    q = a + a1
                    a, a1 = below(3 * c + 2)
                    r = a1 - a
                    pm, p_end = rows_of(p)
                    qm, q_end = rows_of(q)
                    rm, r_end = rows_of(r)
                    u, u_end = p + pm, p_end
                    v, v_end = (qm - q) + (r + rm), q_end + r_end
                    to_low, to_low_end = v - u, v_end - u_end
                    to_high, to_high_end = v + u, v_end + u_end
                else:
                    a, a1 = below(9)
                    p = a + a1
                    pm, p_end = rows_of(p)
                    to_low = to_high = p + pm
                    to_low_end = to_high_end = p_end
                if top:
                    F[s, c, X, 0:Y] = to_high
                    F[s, c, X, Y:YN] = to_high_end
                else:
                    F[s, c, i + 1, 0:Y] = F[s, c, i + 1, 0:Y] + to_high
                    F[s, c, i + 1, Y:YN] = F[s, c, i + 1, Y:YN] + to_high_end
                F[s, c, i, 0:Y] = to_low
                F[s, c, i, Y:YN] = to_low_end

        node_sums(X - 1, True)
        waits.append(shift(F.at[s, 0:comps, X, 0:Y], FRX.at[s, 0:comps], ("gx",), 1))
        for c in range(comps):
            FSXY[s, c:c + 1] = F[s, c, X, Y:YN]
        waits.append(shift(FSXY.at[s], FRXY.at[s], ("gx", "gy"), 1))
        loop(X - 1, lambda k: node_sums(X - 2 - k, False))
        for c in range(comps):
            for i in range(X):
                FSY[s, c * X + i:c * X + i + 1] = F[s, c, i, Y:YN]
        waits.append(shift(FSY.at[s, 0:comps * X], FRY.at[s, 0:comps * X], ("gy",), 1))
        line_min = spread_min(plane_min(), s, 1, line_group, DRX)
        for w in waits:
            w()
        moved = FRZ[s] + pltpu.roll(jnp.where(last_lane, FRXZ[s], 0.0), Z - X, 1)
        GS[0] = moved[0:Y] + jnp.where(row == 0, moved[Y:YN], 0.0)
        for c in range(comps):
            for i in range(X):
                F[s, c, i, 0:1] = F[s, c, i, 0:1] + FRY[s, c * X + i:c * X + i + 1]
            F[s, c, 0, 0:Y] = F[s, c, 0, 0:Y] + FRX[s, c]
            F[s, c, 0, 0:1] = F[s, c, 0, 0:1] + FRXY[s, c:c + 1]

        acc = T if final else ACC

        def accelerate(i):
            def total_of(c):
                ghost = pltpu.roll(GS[0], lax.rem(Z - (c * XN + i), Z), 1)
                return F[s, c, i, 0:Y] + jnp.where(lane == 0, ghost, 0.0)

            if s == 0:
                INVM[i] = 1.0 / total_of(3)
            for c in range(3):
                acc[c, i, 0:Y] = total_of(c) * INVM[i]

        if not final:
            accelerate(0)
            acc_wait = shift(ACC.at[:, 0, 0:Y], ACC.at[:, X, 0:Y], ("gx",), -1)
            loop(X - 1, lambda k: accelerate(k + 1))
            acc_ghosts = ghosts_down(ACC, 1, 3, 3)
        else:
            loop(X, accelerate)
        dt = COURANT * jnp.min(line_min())

        def heat(i):
            eo_ref[i] = eo_ref[i] - dt * ER[i]

        loop(X, heat)
        if not final:
            acc_wait()
            ghost_acc = acc_ghosts()

        one = [flags[k] == 1 for k in range(6)]
        wall_x0 = jnp.where(one[0], start_x, far)
        wall_x1 = jnp.where(one[1], end_x, far)
        wall_y0 = jnp.where(one[2], start_y, far)
        wall_y1 = jnp.where(one[3], end_y, far)
        wall_z0 = jnp.where(one[4], start_z, far)
        wall_z1 = jnp.where(one[5], end_z, far)
        rows = Y if final else YP
        row_n, lane_n = (row, lane) if final else (row_p, lane_p)

        def move(i):
            for c in range(3):
                speed = N[3 + c, i, 0:rows] + dt * acc[c, i, 0:rows]
                if c == 0:
                    on_wall = (i == wall_x0) | (i == wall_x1)
                elif c == 1:
                    on_wall = (row_n == wall_y0) | (row_n == wall_y1)
                else:
                    on_wall = (lane_n == wall_z0) | (lane_n == wall_z1)
                speed = jnp.where(on_wall, 0.0, speed)
                place = N[c, i, 0:rows] + dt * speed
                if final:
                    vo_ref[c, i] = speed
                    do_ref[c, i] = place
                else:
                    N[3 + c, i] = speed
                    N[c, i] = place

        loop(X if final else XN, move)

        if not final:
            ghosts = G[...]
            speed = ghosts + dt * ghost_acc
            base = 3 * XN
            on_x = (lane_p == base + wall_x0) | (lane_p == base + wall_x1)
            on_y = (lane_p >= base + XN) & (lane_p < base + 2 * XN) & (
                (row_p == wall_y0) | (row_p == wall_y1))
            speed = jnp.where(on_x | on_y, 0.0, speed)
            place = ghosts + dt * pltpu.roll(speed, Z - base, 1)
            G[...] = jnp.where(lane_p < base, place, speed)

    for drain in pending:
        drain()


def solution(mesh):
    sizes = tuple(mesh.shape[a] for a in AXES)

    def body(displacement, velocity, energy, density, region, adiabatic, face_flags):
        X, Y, Z = shape = energy.shape
        XN, YP = X + 1, Y + 8
        f32 = jnp.float32
        vm = lambda *dims: pltpu.VMEM(dims, f32)
        plane = max(1, sizes[1] * sizes[2] - 1)
        line = max(1, sizes[0] - 1)
        copies = 2 + 6 + 7 + STEPS * (6 + 7 + plane + line)
        scratch = [
            vm(6, XN, YP, Z), vm(X, Y, Z), pltpu.VMEM((X, Y, Z), jnp.int32),
            pltpu.SMEM(adiabatic.shape, f32), pltpu.SMEM(face_flags.shape, jnp.int32),
            vm(YP, Z), vm(2, Y, Z), vm(18, XN, Y, Z), vm(9, X, Y, Z), vm(X, Y, Z), vm(X, Y, Z),
            vm(X, Y, Z), vm(X, Y, Z), vm(STEPS, X + 2, Y + 16, Z),
            vm(STEPS, 2, up8(X), Z), vm(STEPS, 2, up8(X), Z),
            vm(STEPS, 2, Y, Z), vm(STEPS, 2, Y, Z),
            vm(X, Y, Z), vm(3, XN, YP, Z), vm(STEPS, 4, XN, YP, Z),
            vm(2, up8(6 * X), Z), vm(2, up8(6 * X), Z), vm(2, 8, Z), vm(2, 8, Z),
            vm(2, YP, Z), vm(2, YP, Z), vm(2, YP, Z),
            vm(STEPS, up8(4 * X), Z), vm(STEPS, up8(4 * X), Z), vm(STEPS, 8, Z), vm(STEPS, 8, Z),
            vm(STEPS, YP, Z), vm(STEPS, YP, Z), vm(STEPS, YP, Z), vm(STEPS, 4, Y, Z),
            vm(STEPS, 2, ROWS, Z), vm(STEPS, plane, ROWS, Z), vm(STEPS, line, ROWS, Z),
            pltpu.SemaphoreType.DMA((copies,)), pltpu.SemaphoreType.DMA((copies,)),
            pltpu.SemaphoreType.DMA((7,)),
        ]
        spec_v = pl.BlockSpec(memory_space=pltpu.VMEM)
        spec_a = pl.BlockSpec(memory_space=pl.ANY)
        node = jax.ShapeDtypeStruct(displacement.shape, f32)
        return pl.pallas_call(
            functools.partial(kernel, sizes, shape),
            out_shape=(node, node, jax.ShapeDtypeStruct(energy.shape, f32)),
            in_specs=[spec_a] * 7,
            out_specs=(spec_v, spec_v, spec_v),
            scratch_shapes=scratch,
            compiler_params=pltpu.CompilerParams(
                collective_id=0, has_side_effects=True, vmem_limit_bytes=60000 * 1024),
        )(adiabatic, face_flags, displacement, velocity, energy, density, region)

    node = P(None, "gx", "gy", "gz")
    elem = P("gx", "gy", "gz")
    return jax.shard_map(
        body, mesh=mesh,
        in_specs=(node, node, elem, elem, elem, P(), P()),
        out_specs=(node, node, elem), check_vma=False)
```

```python
import functools

import jax
import jax.numpy as jnp
from jax import lax
from jax.experimental import pallas as pl
from jax.experimental.pallas import tpu as pltpu
from jax.sharding import PartitionSpec as P

STEPS = 2
COURANT = 0.25
MESH = pl.DeviceIdType.MESH
AXES = ("gx", "gy", "gz")
ROWS = 8


def up8(n):
    return -(-n // 8) * 8


def kernel(sizes, shape, adi_ref, flags_ref, d_ref, v_ref, e_ref, rho_ref, reg_ref,
           do_ref, vo_ref, eo_ref,
           N, E, PRE, RHO, REG, adi, flags, G, GS, T, C, VOL, GAM, ER, MA, R, SYB, RYB, SZB, RZB,
           INVM, ACC, F, SY, RY, SXY, RXY, SZ, RZ, RXZ, FSY, FRY, FSXY, FRXY, FSZ, FRZ, FRXZ,
           FRX, DS, DRP, DRX, ssem, rsem, lsem):
    X, Y, Z = shape
    XN, YN, YP = X + 1, Y + 1, Y + 8
    n_of = dict(zip(AXES, sizes))
    me = {a: lax.axis_index(a) for a in AXES}
    first = {a: me[a] == 0 for a in AXES}
    last = {a: me[a] == n_of[a] - 1 for a in AXES}
    count = [0]
    pending = []

    def remote(src, dst, target):
        k = count[0]
        count[0] += 1
        return pltpu.make_async_remote_copy(
            src_ref=src, dst_ref=dst, send_sem=ssem.at[k], recv_sem=rsem.at[k],
            device_id=target, device_id_type=MESH)

    def any_of(ends, axes):
        out = ends[axes[0]]
        for a in axes[1:]:
            out = jnp.logical_or(out, ends[a])
        return out

    def shift(src, dst, axes, step):
        can_send = jnp.logical_not(any_of(last if step == 1 else first, axes))
        can_recv = jnp.logical_not(any_of(first if step == 1 else last, axes))
        copy = remote(src, dst, {a: jnp.clip(me[a] + step, 0, n_of[a] - 1) for a in axes})

        @pl.when(can_send)
        def _():
            copy.start()

        def drain():
            @pl.when(can_send)
            def _():
                copy.wait_send()

        pending.append(drain)

        def arrived():
            @pl.when(can_recv)
            def _():
                copy.wait_recv()

        return arrived

    plane_group = [{"gy": lax.rem(me["gy"] + b, n_of["gy"]), "gz": lax.rem(me["gz"] + c, n_of["gz"])}
                   for b in range(n_of["gy"]) for c in range(n_of["gz"]) if b or c]
    line_group = [{"gx": lax.rem(me["gx"] + a, n_of["gx"])} for a in range(1, n_of["gx"])]

    def spread_min(tile, s, slot, targets, buf):
        DS[s, slot] = tile
        copies = []
        for k, target in enumerate(targets):
            copy = remote(DS.at[s, slot], buf.at[s, k], target)
            copy.start()
            pending.append(copy.wait_send)
            copies.append(copy)

        def result():
            out = tile
            for k, copy in enumerate(copies):
                copy.wait_recv()
                out = jnp.minimum(out, buf[s, k])
            return out

        return result

    def loop(n, f):
        def step(i, carry):
            f(i)
            return carry
        lax.fori_loop(0, n, step, 0)

    locals_ = [
        pltpu.make_async_copy(src, dst, lsem.at[k]) for k, (src, dst) in enumerate((
            (d_ref, N.at[0:3, 0:X, 0:Y]), (v_ref, N.at[3:6, 0:X, 0:Y]),
            (rho_ref, RHO), (reg_ref, REG), (adi_ref, adi), (flags_ref, flags), (e_ref, E)))
    ]
    for copy in locals_:
        copy.start()

    barrier = pltpu.get_barrier_semaphore()
    partners = plane_group + line_group
    arrivals = len(partners)
    for target in partners:
        pl.semaphore_signal(barrier, inc=1, device_id=target, device_id_type=MESH)
    for step in (1, -1):
        for axes in (("gx", "gy"), ("gx", "gz"), AXES):
            there = jnp.logical_not(any_of(last if step == 1 else first, axes))
            arrivals = arrivals + jnp.where(there, 1, 0)
            target = {a: jnp.clip(me[a] + step, 0, n_of[a] - 1) for a in axes}

            @pl.when(there)
            def _():
                pl.semaphore_signal(barrier, inc=1, device_id=target, device_id_type=MESH)

    lane = lax.broadcasted_iota(jnp.int32, (Y, Z), 1)
    lane_p = lax.broadcasted_iota(jnp.int32, (YP, Z), 1)
    row_p = lax.broadcasted_iota(jnp.int32, (YP, Z), 0)
    row = lax.broadcasted_iota(jnp.int32, (Y, Z), 0)
    lane_b = lax.broadcasted_iota(jnp.int32, (ROWS, Z), 1)
    row_b = lax.broadcasted_iota(jnp.int32, (ROWS, Z), 0)
    i32 = lambda b: b.astype(jnp.int32)
    far = 1 << 20
    end_x = jnp.where(last["gx"], X - 1, far)
    end_y = jnp.where(last["gy"], Y - 1, far)
    end_z = jnp.where(last["gz"], Z - 1, far)
    start_x = jnp.where(first["gx"], 0, far)
    start_y = jnp.where(first["gy"], 0, far)
    start_z = jnp.where(first["gz"], 0, far)

    def present_of(i, r0):
        edge = jnp.where(i == end_x, -1, 0)
        rb = row_b + r0
        inside = jnp.where((rb == end_y) | (lane_b == end_z), -1, 0)
        return (inside + edge) == 0

    zeros_p = jnp.zeros((YP, Z), jnp.float32)
    last_lane = lane_p == X
    first_lane = lane_p == 0
    for c in range(1, 6):
        last_lane = last_lane | (lane_p == c * XN + X)

    def clear(condition, *places):
        @pl.when(condition)
        def _():
            for ref, index in places:
                ref[index] = jnp.zeros(ref[index].shape, jnp.float32)

    steps = range(STEPS)
    low_rows, high_rows = slice(0, Y), slice(Y, YP)
    clear(last["gx"], *[(N, (c, X)) for c in range(6)], *[(ACC, (c, X)) for c in range(3)],
          *[(R, (s, X + 1)) for s in steps])
    clear(first["gx"], *[(R, (s, 0)) for s in steps],
          *[(FRX, (s, c)) for s in steps for c in range(4)])
    clear(last["gy"], *[(RY, (k,)) for k in range(2)], *[(RYB, (s, 1)) for s in steps])
    clear(first["gy"], *[(RYB, (s, 0)) for s in steps], *[(FRY, (s,)) for s in steps])
    clear(last["gz"], *[(RZ, (k, low_rows)) for k in range(2)], *[(RZB, (s, 1)) for s in steps])
    clear(first["gz"], *[(RZB, (s, 0)) for s in steps], *[(FRZ, (s, low_rows)) for s in steps])
    for axes, down, rows_down, up, rows_up in (
            (("gx", "gy"), RXY, None, FRXY, None),
            (("gx", "gz"), RXZ, low_rows, FRXZ, low_rows),
            (("gy", "gz"), RZ, high_rows, FRZ, high_rows),
            (AXES, RXZ, high_rows, FRXZ, high_rows)):
        at = lambda k, rows: (k,) if rows is None else (k, rows)
        clear(any_of(last, axes), *[(down, at(k, rows_down)) for k in range(2)])
        clear(any_of(first, axes), *[(up, at(s, rows_up)) for s in steps])

    def ghosts_down(ref, k, comps, base):
        for c in range(comps):
            for i in range(X):
                SY[k, c * X + i:c * X + i + 1] = ref[c, i, 0:1]
            SXY[k, c:c + 1] = ref[c, 0, 0:1]
        packed = jnp.zeros((Y, Z), jnp.float32)
        for c in range(comps):
            for i in range(XN):
                j = (base + c) * XN + i
                value = ref[c, i % X, 0:Y]
                packed = jnp.where(lane == j, pltpu.roll(value, j, 1) if j else value, packed)
        SZ[k, 0:Y] = packed
        SZ[k, Y:YP] = packed[0:8]
        waits = []

        def send():
            waits.extend(
                shift(SZ.at[k, rows], into.at[k, rows], axes, -1)
                for axes, into, rows in ((AXES, RXZ, high_rows), (("gx", "gz"), RXZ, low_rows),
                                         (("gy", "gz"), RZ, high_rows), (("gz",), RZ, low_rows)))
            waits.append(shift(SXY.at[k], RXY.at[k], ("gx", "gy"), -1))
            used = up8(comps * X)
            waits.append(shift(SY.at[k, 0:used], RY.at[k, 0:used], ("gy",), -1))

        def finish():
            for w in waits:
                w()
            for c in range(comps):
                for i in range(X):
                    ref[c, i, Y:YN] = RY[k, c * X + i:c * X + i + 1]
                ref[c, X, Y:YN] = RXY[k, c:c + 1]
            return jnp.where(last_lane, RXZ[k], RZ[k])

        return send, finish

    pl.semaphore_wait(barrier, arrivals)
    node_waits = [shift(d_ref.at[:, 0], N.at[0:3, X, 0:Y], ("gx",), -1),
                  shift(v_ref.at[:, 0], N.at[3:6, X, 0:Y], ("gx",), -1)]
    locals_[0].wait()
    locals_[1].wait()
    send_nodes, node_ghosts = ghosts_down(N, 0, 6, 0)
    send_nodes()
    for copy in locals_[2:]:
        copy.wait()

    def load(i):
        reg = REG[i]
        gam = jnp.zeros((Y, Z), jnp.float32)
        for k in range(adi.shape[0]):
            gam = jnp.where(reg == k, adi[k], gam)
        GAM[i] = gam
        for r0 in range(0, Y, ROWS):
            rs = slice(r0, r0 + ROWS)
            MA[i, rs] = jnp.where(present_of(i, r0), 0.125 * RHO[i, rs], 0.0)

    loop(X, load)
    for w in node_waits:
        w()
    G[...] = node_ghosts()

    for s in range(STEPS):
        final = s == STEPS - 1

        GS[0] = G[0:Y] + G[1:YN]
        GS[1] = G[1:YN] - G[0:Y]

        def plane_sums(i):
            for c in range(6):
                back = Z - 1 - (c * XN + i)
                ghost_s = pltpu.roll(GS[0], back, 1)
                ghost_d = pltpu.roll(GS[1], back, 1)
                low, high = N[c, i, 0:Y], N[c, i, 1:YN]
                ys, yd = low + high, high - low
                ys1 = jnp.where(lane == Z - 1, ghost_s, pltpu.roll(ys, Z - 1, 1))
                yd1 = jnp.where(lane == Z - 1, ghost_d, pltpu.roll(yd, Z - 1, 1))
                T[3 * c, i] = ys + ys1
                T[3 * c + 1, i] = yd + yd1
                T[3 * c + 2, i] = ys1 - ys

        loop(XN, plane_sums)

        def kinematics(i):
            for r0 in range(0, Y, ROWS):
                rs = slice(r0, r0 + ROWS)

                def grad(c):
                    return (
                        0.25 * (T[3 * c, i + 1, rs] - T[3 * c, i, rs]),
                        0.25 * (T[3 * c + 1, i + 1, rs] + T[3 * c + 1, i, rs]),
                        0.25 * (T[3 * c + 2, i + 1, rs] + T[3 * c + 2, i, rs]),
                    )

                jac = [list(grad(c)) for c in range(3)]
                for c in range(3):
                    jac[c][c] = jac[c][c] + 1.0

                def minor(r1, r2, c1, c2):
                    return jac[r1][c1] * jac[r2][c2] - jac[r1][c2] * jac[r2][c1]

                cof = [
                    [minor(1, 2, 1, 2), minor(1, 2, 2, 0), minor(1, 2, 0, 1)],
                    [minor(2, 0, 1, 2), minor(2, 0, 2, 0), minor(2, 0, 0, 1)],
                    [minor(0, 1, 1, 2), minor(0, 1, 2, 0), minor(0, 1, 0, 1)],
                ]
                volume = jac[0][0] * cof[0][0] + jac[0][1] * cof[0][1] + jac[0][2] * cof[0][2]
                change = 0.0
                for c in range(3):
                    rate = grad(3 + c)
                    for e in range(3):
                        change = change + cof[c][e] * rate[e]
                        C[3 * c + e, i, rs] = cof[c][e]
                VOL[i, rs] = volume
                R[s, i + 1, 8 + r0:8 + r0 + ROWS] = change / volume

        loop(X, kinematics)

        own = slice(8, 8 + Y)
        waits = [
            shift(R.at[s, X, own], R.at[s, 0, own], ("gx",), 1),
            shift(R.at[s, 1, own], R.at[s, X + 1, own], ("gx",), -1),
        ]
        for i in range(X):
            SYB[s, 0, i:i + 1] = R[s, i + 1, 7 + Y:8 + Y]
            SYB[s, 1, i:i + 1] = R[s, i + 1, 8:9]
        waits += [
            shift(SYB.at[s, 0], RYB.at[s, 0], ("gy",), 1),
            shift(SYB.at[s, 1], RYB.at[s, 1], ("gy",), -1),
        ]
        to_up = to_down = jnp.zeros((Y, Z), jnp.float32)
        for i in range(X):
            value = R[s, i + 1, own]
            to_up = jnp.where(lane == i, pltpu.roll(value, i + 1, 1), to_up)
            to_down = jnp.where(lane == i, pltpu.roll(value, i, 1) if i else value, to_down)
        SZB[s, 0] = to_up
        SZB[s, 1] = to_down
        waits += [
            shift(SZB.at[s, 0], RZB.at[s, 0], ("gz",), 1),
            shift(SZB.at[s, 1], RZB.at[s, 1], ("gz",), -1),
        ]

        def before_stress(i):
            for r0 in range(0, Y, ROWS):
                rs = slice(r0, r0 + ROWS)
                volume = VOL[i, rs]
                size = jnp.exp(jnp.log(jnp.abs(volume)) * (1.0 / 3.0))
                PRE[0, i, rs] = size * size
                PRE[1, i, rs] = jnp.where(volume < 0.0, -size, size)
                PRE[2, i, rs] = 0.25 * RHO[i, rs] / volume
                PRE[3, i, rs] = (GAM[i, rs] - 1.0) * E[i, rs]

        loop(X, before_stress)
        for w in waits:
            w()
        for i in range(X):
            R[s, i + 1, 7:8] = RYB[s, 0, i:i + 1]
            R[s, i + 1, 8 + Y:9 + Y] = RYB[s, 1, i:i + 1]

        is_one = [jnp.where(flags[k] == 1, 1.0, 0.0) for k in range(6)]

        def stresses(i, least):
            low_x, high_x = i == start_x, i == end_x - 1
            for r0 in range(0, Y, ROWS):
                rs = slice(r0, r0 + ROWS)
                rr = slice(8 + r0, 8 + r0 + ROWS)
                rate = R[s, i + 1, rr]
                rb = row_b + r0
                present = present_of(i, r0)
                xl = jnp.where(low_x, is_one[0] * rate, R[s, i, rr])
                xu = jnp.where(high_x, is_one[1] * rate, R[s, i + 2, rr])
                yl = jnp.where(rb == start_y, is_one[2] * rate,
                               R[s, i + 1, 7 + r0:7 + r0 + ROWS])
                yu = jnp.where(rb == end_y - 1, is_one[3] * rate,
                               R[s, i + 1, 9 + r0:9 + r0 + ROWS])
                ghost_l = pltpu.roll(RZB[s, 0, rs], lax.rem(Z - i, Z), 1)
                ghost_u = pltpu.roll(RZB[s, 1, rs], Z - 1 - i, 1)
                zl = jnp.where(lane_b == 0, ghost_l, pltpu.roll(rate, 1, 1))
                zu = jnp.where(lane_b == Z - 1, ghost_u, pltpu.roll(rate, Z - 1, 1))
                zl = jnp.where(lane_b == start_z, is_one[4] * rate, zl)
                zu = jnp.where(lane_b == end_z - 1, is_one[5] * rate, zu)
                rough = 0.0
                for lo, hi in ((xl, xu), (yl, yu), (zl, zu)):
                    f, g = hi - rate, rate - lo
                    rough = rough + jnp.abs(
                        jnp.maximum(jnp.minimum(f, g), 0.0) + jnp.minimum(jnp.maximum(f, g), 0.0))
                ge = PRE[3, i, rs]
                compress = jnp.maximum(-rate, 0.0)
                visc = PRE[0, i, rs] * compress * (compress + rough)
                work = jnp.where(present, ge + visc, 0.0)
                ratio = PRE[1, i, rs] * lax.rsqrt(GAM[i, rs] * ge + visc)
                least = jnp.minimum(least, jnp.where(present, ratio, jnp.inf))
                ER[i, rs] = jnp.where(present, work * rate, 0.0)
                quarter = jnp.where(present, work * PRE[2, i, rs], 0.0)
                for q in range(9):
                    C[q, i, rs] = quarter * C[q, i, rs]
            return least

        least = lax.fori_loop(0, X, stresses, jnp.full((ROWS, Z), jnp.inf, jnp.float32))

        plane_min = spread_min(least, s, 0, plane_group, DRP)
        comps = 3 if s else 4

        def column_pack(i, tiles):
            out = []
            for part, tile in enumerate(tiles):
                for c in range(comps):
                    if c == 3 and part != 2:
                        continue
                    value = MA[i] if c == 3 else C[3 * c + part, i]
                    j = c * XN + i
                    tile = jnp.where(lane == j, pltpu.roll(value, lax.rem(j + 1, Z), 1), tile)
                out.append(tile)
            return tuple(out)

        tiles = lax.fori_loop(0, X, column_pack, (jnp.zeros((Y, Z), jnp.float32),) * 3)
        p, q, r = [jnp.concatenate([t, jnp.zeros((8, Z), jnp.float32)], 0) for t in tiles]
        pm, qm, rm = [pltpu.roll(t, 1, 0) for t in (p, q, r)]
        u, v = p + pm, (qm - q) + (r + rm)
        FSZ[s] = (v - u) + pltpu.roll(v + u, 1, 1)
        waits = [shift(FSZ.at[s, rows], into.at[s, rows], axes, 1)
                 for axes, into, rows in ((AXES, FRXZ, high_rows), (("gx", "gz"), FRXZ, low_rows),
                                          (("gy", "gz"), FRZ, high_rows), (("gz",), FRZ, low_rows))]

        def node_sums(i, top):
            def below(q):
                value = C[q, i] if q < 9 else MA[i]
                return value, jnp.where(lane == 0, 0.0, pltpu.roll(value, 1, 1))

            def rows_of(value):
                moved = pltpu.roll(value, 1, 0)
                return jnp.where(row == 0, 0.0, moved), moved[0:1]

            for c in range(comps):
                if c < 3:
                    a, a1 = below(3 * c)
                    p = a + a1
                    a, a1 = below(3 * c + 1)
                    q = a + a1
                    a, a1 = below(3 * c + 2)
                    r = a1 - a
                    pm, p_end = rows_of(p)
                    qm, q_end = rows_of(q)
                    rm, r_end = rows_of(r)
                    u, u_end = p + pm, p_end
                    v, v_end = (qm - q) + (r + rm), q_end + r_end
                    to_low, to_low_end = v - u, v_end - u_end
                    to_high, to_high_end = v + u, v_end + u_end
                else:
                    a, a1 = below(9)
                    p = a + a1
                    pm, p_end = rows_of(p)
                    to_low = to_high = p + pm
                    to_low_end = to_high_end = p_end
                if top:
                    F[s, c, X, 0:Y] = to_high
                    F[s, c, X, Y:YN] = to_high_end
                else:
                    F[s, c, i + 1, 0:Y] = F[s, c, i + 1, 0:Y] + to_high
                    F[s, c, i + 1, Y:YN] = F[s, c, i + 1, Y:YN] + to_high_end
                F[s, c, i, 0:Y] = to_low
                F[s, c, i, Y:YN] = to_low_end

        node_sums(X - 1, True)
        waits.append(shift(F.at[s, 0:comps, X, 0:Y], FRX.at[s, 0:comps], ("gx",), 1))
        for c in range(comps):
            FSXY[s, c:c + 1] = F[s, c, X, Y:YN]
        waits.append(shift(FSXY.at[s], FRXY.at[s], ("gx", "gy"), 1))
        loop(X - 1, lambda k: node_sums(X - 2 - k, False))
        for c in range(comps):
            for i in range(X):
                FSY[s, c * X + i:c * X + i + 1] = F[s, c, i, Y:YN]
        waits.append(shift(FSY.at[s, 0:comps * X], FRY.at[s, 0:comps * X], ("gy",), 1))
        line_min = spread_min(plane_min(), s, 1, line_group, DRX)
        for w in waits:
            w()
        moved = FRZ[s] + pltpu.roll(jnp.where(last_lane, FRXZ[s], 0.0), Z - X, 1)
        GS[0] = moved[0:Y] + jnp.where(row == 0, moved[Y:YN], 0.0)
        for c in range(comps):
            for i in range(X):
                F[s, c, i, 0:1] = F[s, c, i, 0:1] + FRY[s, c * X + i:c * X + i + 1]
            F[s, c, 0, 0:Y] = F[s, c, 0, 0:Y] + FRX[s, c]
            F[s, c, 0, 0:1] = F[s, c, 0, 0:1] + FRXY[s, c:c + 1]

        one = [flags[k] == 1 for k in range(6)]
        wall_x0 = jnp.where(one[0], start_x, far)
        wall_x1 = jnp.where(one[1], end_x, far)
        wall_y0 = jnp.where(one[2], start_y, far)
        wall_y1 = jnp.where(one[3], end_y, far)
        wall_z0 = jnp.where(one[4], start_z, far)
        wall_z1 = jnp.where(one[5], end_z, far)

        def on_wall(c, i, row_n, lane_n):
            if c == 0:
                return (i == wall_x0) | (i == wall_x1)
            if c == 1:
                return (row_n == wall_y0) | (row_n == wall_y1)
            return (lane_n == wall_z0) | (lane_n == wall_z1)

        acc = T if final else ACC

        def accelerate(i):
            def total_of(c):
                ghost = pltpu.roll(GS[0], lax.rem(Z - (c * XN + i), Z), 1)
                return F[s, c, i, 0:Y] + jnp.where(lane == 0, ghost, 0.0)

            if s == 0:
                INVM[i] = 1.0 / total_of(3)
            for c in range(3):
                value = total_of(c) * INVM[i]
                if final:
                    value = jnp.where(on_wall(c, i, row, lane), 0.0, value)
                acc[c, i, 0:Y] = value

        if not final:
            accelerate(0)
            acc_wait = shift(ACC.at[:, 0, 0:Y], ACC.at[:, X, 0:Y], ("gx",), -1)
            loop(X - 1, lambda k: accelerate(k + 1))
            send_acc, acc_ghosts = ghosts_down(ACC, 1, 3, 3)
            send_acc()
        else:
            loop(X, accelerate)
        dt = COURANT * jnp.min(line_min())
        if final:
            def finish(i):
                for c in range(3):
                    speed = N[3 + c, i, 0:Y] + dt * acc[c, i, 0:Y]
                    vo_ref[c, i] = speed
                    do_ref[c, i] = N[c, i, 0:Y] + dt * speed
                eo_ref[i] = E[i] - dt * ER[i]

            loop(X, finish)
            break

        def heat(i):
            E[i] = E[i] - dt * ER[i]

        def move(i, rs, row_n, lane_n):
            for c in range(3):
                speed = N[3 + c, i, rs] + dt * ACC[c, i, rs]
                speed = jnp.where(on_wall(c, i, row_n, lane_n), 0.0, speed)
                N[3 + c, i, rs] = speed
                N[c, i, rs] = N[c, i, rs] + dt * speed

        own_rows, ghost_rows = slice(0, Y), slice(Y, YP)
        loop(X, lambda i: move(i, own_rows, row, lane))
        loop(X, heat)
        acc_wait()
        ghost_acc = acc_ghosts()
        move(X, own_rows, row, lane)
        loop(XN, lambda i: move(i, ghost_rows, row_b + Y, lane_b))

        ghosts = G[...]
        speed = ghosts + dt * ghost_acc
        base = 3 * XN
        on_x = (lane_p == base + wall_x0) | (lane_p == base + wall_x1)
        on_y = (lane_p >= base + XN) & (lane_p < base + 2 * XN) & (
            (row_p == wall_y0) | (row_p == wall_y1))
        speed = jnp.where(on_x | on_y, 0.0, speed)
        place = ghosts + dt * pltpu.roll(speed, Z - base, 1)
        G[...] = jnp.where(lane_p < base, place, speed)

    for drain in pending:
        drain()


def solution(mesh):
    sizes = tuple(mesh.shape[a] for a in AXES)

    def body(displacement, velocity, energy, density, region, adiabatic, face_flags):
        X, Y, Z = shape = energy.shape
        XN, YP = X + 1, Y + 8
        f32 = jnp.float32
        vm = lambda *dims: pltpu.VMEM(dims, f32)
        plane = max(1, sizes[1] * sizes[2] - 1)
        line = max(1, sizes[0] - 1)
        copies = 2 + 6 + 7 + STEPS * (6 + 7 + plane + line)
        scratch = [
            vm(6, XN, YP, Z), vm(X, Y, Z), vm(4, X, Y, Z), vm(X, Y, Z), pltpu.VMEM((X, Y, Z), jnp.int32),
            pltpu.SMEM(adiabatic.shape, f32), pltpu.SMEM(face_flags.shape, jnp.int32),
            vm(YP, Z), vm(2, Y, Z), vm(18, XN, Y, Z), vm(9, X, Y, Z), vm(X, Y, Z), vm(X, Y, Z),
            vm(X, Y, Z), vm(X, Y, Z), vm(STEPS, X + 2, Y + 16, Z),
            vm(STEPS, 2, up8(X), Z), vm(STEPS, 2, up8(X), Z),
            vm(STEPS, 2, Y, Z), vm(STEPS, 2, Y, Z),
            vm(X, Y, Z), vm(3, XN, YP, Z), vm(STEPS, 4, XN, YP, Z),
            vm(2, up8(6 * X), Z), vm(2, up8(6 * X), Z), vm(2, 8, Z), vm(2, 8, Z),
            vm(2, YP, Z), vm(2, YP, Z), vm(2, YP, Z),
            vm(STEPS, up8(4 * X), Z), vm(STEPS, up8(4 * X), Z), vm(STEPS, 8, Z), vm(STEPS, 8, Z),
            vm(STEPS, YP, Z), vm(STEPS, YP, Z), vm(STEPS, YP, Z), vm(STEPS, 4, Y, Z),
            vm(STEPS, 2, ROWS, Z), vm(STEPS, plane, ROWS, Z), vm(STEPS, line, ROWS, Z),
            pltpu.SemaphoreType.DMA((copies,)), pltpu.SemaphoreType.DMA((copies,)),
            pltpu.SemaphoreType.DMA((7,)),
        ]
        spec_v = pl.BlockSpec(memory_space=pltpu.VMEM)
        spec_a = pl.BlockSpec(memory_space=pl.ANY)
        node = pltpu.VMEM(displacement.shape, f32)
        return pl.pallas_call(
            functools.partial(kernel, sizes, shape),
            out_shape=(node, node, pltpu.VMEM(energy.shape, f32)),
            in_specs=[spec_a] * 7,
            out_specs=(spec_v,) * 3,
            scratch_shapes=scratch,
            compiler_params=pltpu.CompilerParams(
                collective_id=0, has_side_effects=True, vmem_limit_bytes=60000 * 1024),
        )(adiabatic, face_flags, displacement, velocity, energy, density, region)

    node = P(None, "gx", "gy", "gz")
    elem = P("gx", "gy", "gz")
    return jax.shard_map(
        body, mesh=mesh,
        in_specs=(node, node, elem, elem, elem, P(), P()),
        out_specs=(node, node, elem), check_vma=False)
```
